512 devices in a mesh: sec: 16 (over y, core), op: 32 (over z, x).
Axes of the slice: x: 4, y: 8, z: 8, core: 2. Of those that a mesh axis runs over, the one named last changes fastest.
Arguments:
- wavefunction: bfloat16 [16, 2, 384, 384], P('sec', None, 'op'), may hold values from -6 to 6
- diagonal: float32 [16, 384, 384], P('sec', 'op'), may hold values from 0.5 to 2
- left_ops: bfloat16 [2048, 384, 384], P(('sec', 'op')), may hold values from -0.01953125 to 0.01953125
- right_ops: bfloat16 [2048, 384, 384], P(('sec', 'op')), may hold values from -0.3125 to 0.3125
- offsets: int32 [2048, 2], P(('sec', 'op')), may hold values from 0 to 1
Outputs:
- preconditioned: bfloat16 [16, 2, 384, 384], P('sec', None, 'op')
The draws below stay inside these ranges and needn't reach their ends.
All inputs are finite; a program needn't handle non-finite values.
Results may differ from the reference program's by a relative error of at most 0.025.
Values may be sent and summed in bfloat16 or wider, within the bound.
A program may use at most 64 MiB of HBM per device.

```python
import math
import jax
import jax.numpy as jnp
from jax import lax

B = 384
ROOTS = 2
PAIRS = 4
ITERS = 2
SECTORS = 16
GROUP_PAIRS = 128
PAIRS_ALL = 2048
N_OP = 32


def with_ends(entries, key, low, largest):
    spot = [jax.random.randint(jax.random.fold_in(key, axis), (), 0, length) for axis, length in enumerate(entries.shape)]
    widest = entries.shape.index(max(entries.shape))
    beside = spot[:widest] + [(spot[widest] + 1) % entries.shape[widest]] + spot[widest + 1:]
    return entries.at[tuple(spot)].set(low).at[tuple(beside)].set(largest)


def block_levels(rng, shape, pieces, smallest, largest):
    def one(position, blocks):
        steps = jax.random.uniform(jax.random.fold_in(jax.random.fold_in(rng, 6), position), (blocks,), jnp.float32, smallest / len(pieces), largest / len(pieces))
        return jnp.repeat(jnp.exp(steps), shape[position] // blocks).reshape((-1,) + (1,) * (len(shape) - position - 1))

    factor_of = one(*pieces[0])
    for cut in pieces[1:]:
        factor_of = factor_of * one(*cut)
    return factor_of


def normal_values(rng, shape, scale, most, pieces=(), kind=jnp.bfloat16):
    factor_of = block_levels(rng, shape, pieces, -0.22, 0.18) if pieces else 1.0
    entries = jax.random.normal(rng, shape, jnp.float32) * scale * factor_of
    return jnp.minimum(jnp.maximum(entries, -most), most).astype(kind)


def setup_inputs(seed: int = 0) -> dict:
    key_list = jax.random.split(jax.random.key(seed), 6)
    wavefunction = normal_values(key_list[0], (SECTORS, ROOTS, B, B), 1.0, 6.0, ((0, 16), (2, 32)))
    diagonal = jnp.clip(jnp.exp(math.log(2.0) - 1.3862944 * jax.random.uniform(key_list[1], (SECTORS, B, B), jnp.float32) ** block_levels(key_list[1], (SECTORS, B, B), ((0, 16), (1, 32)), -0.2, 0.2)), 0.5, 2.0)
    left_ops = normal_values(key_list[2], (PAIRS_ALL, B, B), (2 * B * GROUP_PAIRS) ** -0.5, 0.01953125, ((0, 512),))
    right_ops = normal_values(key_list[3], (PAIRS_ALL, B, B), B ** -0.5, 0.3125, ((0, 512),))
    offsets = with_ends(jax.random.randint(key_list[4], (PAIRS_ALL, 2), 0, 2), jax.random.fold_in(key_list[4], 1), 0, 1).astype(jnp.int32)
    return {"wavefunction": wavefunction, "diagonal": diagonal, "left_ops": left_ops, "right_ops": right_ops, "offsets": offsets}


def partials(vector, left_ops, right_ops, offsets):
    vector_f = vector.astype(jnp.float32)
    right_f = right_ops.astype(jnp.float32)
    left_f = left_ops.astype(jnp.float32)
    turned = jnp.einsum('xab,pcb->pxac', vector_f, right_f).astype(jnp.bfloat16).astype(jnp.float32)
    plain_rows = jnp.einsum('xab,pbc->pxac', vector_f, right_f).astype(jnp.bfloat16).astype(jnp.float32)
    raise_mask = (offsets[:, 0] == 1).astype(jnp.float32)[:, None, None]
    lower_mask = (offsets[:, 1] == 1).astype(jnp.float32)[:, None, None]
    raised = jnp.einsum('pab,pxbc->xac', left_f * raise_mask, turned)
    staying = jnp.einsum('pab,pxbc->xac', left_f * (1.0 - raise_mask), turned)
    staying = staying + jnp.einsum('pba,pxbc->xac', left_f * (1.0 - lower_mask), plain_rows)
    lowered = jnp.einsum('pba,pxbc->xac', left_f * lower_mask, plain_rows)
    return jnp.stack([lowered.astype(jnp.bfloat16), staying.astype(jnp.bfloat16), raised.astype(jnp.bfloat16)])


def apply_sigma(vectors, left_ops, right_ops, offsets):
    groups = PAIRS_ALL // PAIRS

    def add_group(accumulated, group):
        sector = (group // N_OP).astype(jnp.int32)
        first = (group * PAIRS).astype(jnp.int32)
        left_group = lax.dynamic_slice_in_dim(left_ops, first, PAIRS, 0)
        right_group = lax.dynamic_slice_in_dim(right_ops, first, PAIRS, 0)
        offset_group = lax.dynamic_slice_in_dim(offsets, first, PAIRS, 0)
        vector = lax.dynamic_index_in_dim(vectors, sector, 0, keepdims=False)
        stacked = partials(vector, left_group, right_group, offset_group).astype(jnp.float32)
        current = lax.dynamic_slice_in_dim(accumulated, sector, 3, 0)
        return lax.dynamic_update_slice_in_dim(accumulated, current + stacked, sector, 0), None

    start = jnp.zeros((SECTORS + 2, ROOTS, B, B), jnp.float32)
    accumulated, _ = lax.scan(add_group, start, jnp.arange(groups, dtype=jnp.int32))
    return accumulated[1:-1]


def reference(wavefunction, diagonal, left_ops, right_ops, offsets):
    vectors = wavefunction
    for turn in range(ITERS):
        sigma = apply_sigma(vectors, left_ops, right_ops, offsets)
        vectors = (sigma / diagonal[:, None]).astype(jnp.bfloat16)
    return vectors
```

```python
import functools

import jax
import jax.numpy as jnp
from jax import lax
from jax.experimental import pallas as pl
from jax.experimental.pallas import tpu as pltpu
from jax.sharding import PartitionSpec as P

ITERS = 2
ROOTS = 2
NX = 4
MESH = pl.DeviceIdType.MESH
F32 = jnp.float32
BF16 = jnp.bfloat16


def dot(a, b):
    return jnp.dot(a, b, preferred_element_type=F32)


def dot_nt(a, b):
    return lax.dot_general(a, b, (((1,), (1,)), ((), ())), preferred_element_type=F32)


def remote(src, dst, send, recv, device):
    return pltpu.make_async_remote_copy(
        src_ref=src, dst_ref=dst, send_sem=send, recv_sem=recv, device_id=device, device_id_type=MESH
    )


def kernel(
    ns, nz, wave, diagonal, left_hbm, right_hbm, offsets, out,
    left, right, perm, first, second, halves, pieces, rows, stay, cross_out, cross_in,
    far_out, far_in, near_out, near_in, share_out, share_in, chunk_buf,
    load_sem, gz_s, gz_r, gx_s, gx_r, y_s, y_r, xa_s, xa_r, xb_s, xb_r, z_s, z_r,
):
    npairs, size = left.shape[0], left.shape[1]
    chunk = size // NX
    half = chunk // 2
    piece = chunk // nz

    s = lax.axis_index("sec")
    o = lax.axis_index("op")
    z = o // NX
    x = o % NX
    right_x, left_x, far_x = (x + 1) % NX, (x + NX - 1) % NX, (x + 2) % NX
    right_dev = (s, z * NX + right_x)
    left_dev = (s, z * NX + left_x)
    has_up, has_down = s < ns - 1, s > 0
    up_dev, down_dev = (s + 1, o), (s - 1, o)

    def z_peer(d):
        return (z + d) % nz

    def z_dev(d):
        return (s, z_peer(d) * NX + x)

    load_l = pltpu.make_async_copy(left_hbm, left, load_sem.at[0])
    load_r = pltpu.make_async_copy(right_hbm, right, load_sem.at[1])
    load_l.start()
    load_r.start()

    for r in range(ROOTS):
        pieces[0, r, z] = wave[0, r]

    barrier = pltpu.get_barrier_semaphore()
    for d in range(1, nz):
        pl.semaphore_signal(barrier, inc=1, device_id=z_dev(d), device_id_type=MESH)
    pl.semaphore_signal(barrier, inc=1, device_id=right_dev, device_id_type=MESH)
    pl.semaphore_signal(barrier, inc=1, device_id=left_dev, device_id_type=MESH)

    for other in ((s + 1) % ns, (s + ns - 1) % ns):
        pl.semaphore_signal(barrier, inc=1, device_id=(other, o), device_id_type=MESH)
    pl.semaphore_wait(barrier, nz + 3)

    def gz_copy(it, r, d):
        slot = pieces.at[it, r, z]
        return remote(slot, slot, gz_s.at[it, r, d - 1], gz_r.at[it, r, d - 1], z_dev(d))

    def gz_wait(it, r, d):
        slot = pieces.at[it, r, z_peer(nz - d)]
        remote(slot, slot, gz_s.at[it, r, d - 1], gz_r.at[it, r, d - 1], z_dev(d)).wait_recv()

    order = sorted(range(1, nz), key=lambda d: -min(d, nz - d))

    def gather_z_send(it, r):
        for d in order:
            gz_copy(it, r, d).start()

    def gx_copy(it, r, which):
        slot = (
            rows.at[it, r, x],
            rows.at[it, r, x],
            rows.at[it, r, left_x, pl.ds(0, half)],
            rows.at[it, r, right_x, pl.ds(half, half)],
        )[which]
        device = right_dev if which % 2 == 0 else left_dev
        return remote(slot, slot, gx_s.at[it, r, which], gx_r.at[it, r, which], device)

    def gx_wait(it, r, which):
        slot = (
            rows.at[it, r, left_x],
            rows.at[it, r, right_x],
            rows.at[it, r, far_x, pl.ds(0, half)],
            rows.at[it, r, far_x, pl.ds(half, half)],
        )[which]
        device = right_dev if which % 2 == 0 else left_dev
        remote(slot, slot, gx_s.at[it, r, which], gx_r.at[it, r, which], device).wait_recv()

    def gather_x_send(it, r):
        for d in reversed(order):
            gz_wait(it, r, d)
        for k in range(nz):
            chunk_buf[piece * k : piece * (k + 1), :] = pieces[it, r, k].astype(F32)
        rows[it, r, x] = chunk_buf[...].astype(BF16)
        gx_copy(it, r, 0).start()
        gx_copy(it, r, 1).start()

    def gather_x_forward(it, r):
        gx_wait(it, r, 0)
        gx_copy(it, r, 2).start()
        gx_wait(it, r, 1)
        gx_copy(it, r, 3).start()

    def prepare():
        shape = (size, size)
        position = lax.broadcasted_iota(jnp.int32, shape, 0)
        column = lax.broadcasted_iota(jnp.int32, shape, 1)
        x_part = jnp.zeros(shape, jnp.int32)
        for k in range(1, NX):
            x_part = x_part + jnp.where(position >= chunk * k, 1, 0)
        inside = position - chunk * x_part
        z_part = jnp.zeros(shape, jnp.int32)
        for k in range(1, nz):
            z_part = z_part + jnp.where(inside >= piece * k, 1, 0)
        source = (inside - piece * z_part) + piece * x_part + (NX * piece) * z_part
        perm[...] = jnp.where(source == column, 1.0, 0.0).astype(BF16)
        perm_eye = jnp.where(position == column, 1.0, 0.0).astype(BF16)
        load_r.wait()
        for p in range(npairs):
            first[p] = dot_nt(perm_eye, right[p]).astype(BF16)
            first[npairs + p] = right[p]
        load_l.wait()
        for p in range(npairs):
            up = offsets[p, 0].astype(F32)
            down = offsets[p, 1].astype(F32)
            turned_rows = dot(perm[...], left[p]).astype(BF16)
            direct = dot_nt(turned_rows, perm[...])
            cols = slice(size * p, size * (p + 1))
            second[0, :, cols] = (direct * (1.0 - up)).astype(BF16)
            second[1, :, cols] = (direct * up).astype(BF16)
            transposed = dot_nt(perm[...], turned_rows)
            second[2, :, cols] = (transposed * (1.0 - down)).astype(BF16)
            second[3, :, cols] = (transposed * down).astype(BF16)

        blank = jnp.zeros((NX, chunk, size), BF16)

        @pl.when(s == 0)
        def _():
            for it in range(ITERS):
                for r in range(ROOTS):
                    cross_in[it, r, 0] = blank

        @pl.when(s == ns - 1)
        def _():
            for it in range(ITERS):
                for r in range(ROOTS):
                    cross_in[it, r, 1] = blank

    def y_copy(it, r, way, q):
        return remote(
            cross_out.at[it, r, way, q], cross_in.at[it, r, way, q],
            y_s.at[it, r, way, q], y_r.at[it, r, way, q], up_dev if way == 0 else down_dev,
        )

    def y_wait(it, r, q):
        @pl.when(has_down)
        def _():
            y_copy(it, r, 0, q).wait_recv()

        @pl.when(has_up)
        def _():
            y_copy(it, r, 1, q).wait_recv()

    def compute(it, r):
        gx_wait(it, r, 2)
        gx_wait(it, r, 3)
        vector = rows[it, r].reshape(size, size)

        def stage_one(i, carry):
            halves[i] = dot(vector, first[i]).astype(BF16)
            return carry

        lax.fori_loop(0, 2 * npairs, stage_one, 0)
        turned = halves[:npairs].reshape(npairs * size, size)
        plain = halves[npairs:].reshape(npairs * size, size)
        cross_out[it, r, 0] = dot(second[1], turned).astype(BF16).reshape(NX, chunk, size)
        cross_out[it, r, 1] = dot(second[3], plain).astype(BF16).reshape(NX, chunk, size)

        @pl.when(has_up)
        def _():
            for q in (far_x, right_x, left_x, x):
                y_copy(it, r, 0, q).start()

        @pl.when(has_down)
        def _():
            for q in (far_x, right_x, left_x, x):
                y_copy(it, r, 1, q).start()

        stay[r] = dot(second[0], turned).reshape(NX, chunk, size)
        stay[r] = stay[r] + dot(second[2], plain).reshape(NX, chunk, size)

    def total(it, r, q):
        y_wait(it, r, q)
        return stay[r, q] + cross_in[it, r, 0, q].astype(F32) + cross_in[it, r, 1, q].astype(F32)

    def xa_copy(it, r, way):
        return remote(
            far_out.at[it, r, way], far_in.at[it, r, way],
            xa_s.at[it, r, way], xa_r.at[it, r, way], right_dev if way == 0 else left_dev,
        )

    def xb_copy(it, r, way):
        return remote(
            near_out.at[it, r, way], near_in.at[it, r, way],
            xb_s.at[it, r, way], xb_r.at[it, r, way], right_dev if way == 0 else left_dev,
        )

    def reduce_x_far(it, r):
        block = total(it, r, far_x)
        far_out[it, r, 0] = block[:half].astype(BF16)
        far_out[it, r, 1] = block[half:].astype(BF16)
        xa_copy(it, r, 0).start()
        xa_copy(it, r, 1).start()

    def reduce_x_near(it, r):
        block = total(it, r, right_x)
        near_out[it, r, 0, half:] = block[half:].astype(BF16)
        xa_copy(it, r, 0).wait_recv()
        near_out[it, r, 0, :half] = (block[:half] + far_in[it, r, 0].astype(F32)).astype(BF16)
        xb_copy(it, r, 0).start()
        block = total(it, r, left_x)
        near_out[it, r, 1, :half] = block[:half].astype(BF16)
        xa_copy(it, r, 1).wait_recv()
        near_out[it, r, 1, half:] = (block[half:] + far_in[it, r, 1].astype(F32)).astype(BF16)
        xb_copy(it, r, 1).start()
        stay[r, x] = total(it, r, x)

    def z_copy(it, r, d):
        return remote(
            share_out.at[it, r, z_peer(d)], share_in.at[it, r, z],
            z_s.at[it, r, d - 1], z_r.at[it, r, d - 1], z_dev(d),
        )

    def z_wait(it, r, d):
        remote(
            share_out.at[it, r, z_peer(d)], share_in.at[it, r, z_peer(nz - d)],
            z_s.at[it, r, d - 1], z_r.at[it, r, d - 1], z_dev(d),
        ).wait_recv()

    def reduce_z_send(it, r):
        xb_copy(it, r, 0).wait_recv()
        xb_copy(it, r, 1).wait_recv()
        chunk_buf[...] = stay[r, x] + near_in[it, r, 0].astype(F32) + near_in[it, r, 1].astype(F32)
        for k in range(nz):
            share_out[it, r, k] = chunk_buf[piece * k : piece * (k + 1), :].astype(BF16)
        for d in order:
            z_copy(it, r, d).start()
        share_in[it, r, z] = share_out[it, r, z]

    def finish(it, r):
        for d in reversed(order):
            z_wait(it, r, d)
        sigma = share_in[it, r, 0].astype(F32)
        for k in range(1, nz):
            sigma = sigma + share_in[it, r, k].astype(F32)
        result = (sigma / diagonal[0]).astype(BF16)
        if it < ITERS - 1:
            pieces[it + 1, r, z] = result
            gather_z_send(it + 1, r)
        else:
            out[0, r] = result

    both = range(ROOTS)
    for r in both:
        gather_z_send(0, r)
    prepare()
    for it in range(ITERS):
        for r in both:
            gather_x_send(it, r)
        for r in both:
            gather_x_forward(it, r)
        for r in both:
            compute(it, r)
        for r in both:
            reduce_x_far(it, r)
        for r in both:
            reduce_x_near(it, r)
        for r in both:
            reduce_z_send(it, r)
        for r in both:
            finish(it, r)

    for it in range(ITERS):
        for r in both:
            for d in order:
                gz_copy(it, r, d).wait_send()
                z_copy(it, r, d).wait_send()
            for which in range(4):
                gx_copy(it, r, which).wait_send()
            for way in range(2):
                xa_copy(it, r, way).wait_send()
                xb_copy(it, r, way).wait_send()

            @pl.when(has_up)
            def _():
                for q in range(NX):
                    y_copy(it, r, 0, q).wait_send()

            @pl.when(has_down)
            def _():
                for q in range(NX):
                    y_copy(it, r, 1, q).wait_send()


def on_device(ns, nz, wavefunction, diagonal, left_ops, right_ops, offsets):
    npairs, size, _ = left_ops.shape
    chunk = size // NX
    half = chunk // 2
    piece = chunk // nz
    it2 = (ITERS, ROOTS)
    dma = pltpu.SemaphoreType.DMA
    vmem = pl.BlockSpec(memory_space=pltpu.VMEM)
    return pl.pallas_call(
        functools.partial(kernel, ns, nz),
        out_shape=jax.ShapeDtypeStruct(wavefunction.shape, BF16),
        in_specs=[
            vmem, vmem, pl.BlockSpec(memory_space=pl.ANY), pl.BlockSpec(memory_space=pl.ANY),
            pl.BlockSpec(memory_space=pltpu.SMEM),
        ],
        out_specs=vmem,
        scratch_shapes=[
            pltpu.VMEM((npairs, size, size), BF16),
            pltpu.VMEM((npairs, size, size), BF16),
            pltpu.VMEM((size, size), BF16),
            pltpu.VMEM((2 * npairs, size, size), BF16),
            pltpu.VMEM((4, size, npairs * size), BF16),
            pltpu.VMEM((2 * npairs, size, size), BF16),
            pltpu.VMEM(it2 + (nz, piece, size), BF16),
            pltpu.VMEM(it2 + (NX, chunk, size), BF16),
            pltpu.VMEM((ROOTS, NX, chunk, size), F32),
            pltpu.VMEM(it2 + (2, NX, chunk, size), BF16),
            pltpu.VMEM(it2 + (2, NX, chunk, size), BF16),
            pltpu.VMEM(it2 + (2, half, size), BF16),
            pltpu.VMEM(it2 + (2, half, size), BF16),
            pltpu.VMEM(it2 + (2, chunk, size), BF16),
            pltpu.VMEM(it2 + (2, chunk, size), BF16),
            pltpu.VMEM(it2 + (nz, piece, size), BF16),
            pltpu.VMEM(it2 + (nz, piece, size), BF16),
            pltpu.VMEM((chunk, size), F32),
            dma((2,)),
            dma(it2 + (nz - 1,)), dma(it2 + (nz - 1,)),
            dma(it2 + (4,)), dma(it2 + (4,)),
            dma(it2 + (2, NX)), dma(it2 + (2, NX)),
            dma(it2 + (2,)), dma(it2 + (2,)),
            dma(it2 + (2,)), dma(it2 + (2,)),
            dma(it2 + (nz - 1,)), dma(it2 + (nz - 1,)),
        ],
        compiler_params=pltpu.CompilerParams(
            collective_id=0, has_side_effects=True, vmem_limit_bytes=60000 * 1024
        ),
        name="sigma_twice",
    )(wavefunction, diagonal, left_ops, right_ops, offsets)


def solution(mesh):
    in_specs = (
        P("sec", None, "op", None),
        P("sec", "op", None),
        P(("sec", "op"), None, None),
        P(("sec", "op"), None, None),
        P(("sec", "op"), None),
    )
    out_specs = P("sec", None, "op", None)
    body = functools.partial(on_device, mesh.shape["sec"], mesh.shape["op"] // NX)
    return jax.shard_map(
        body, mesh=mesh, in_specs=in_specs, out_specs=out_specs, check_vma=False
    )
```

```python
import functools

import jax
import jax.numpy as jnp
from jax import lax
from jax.experimental import pallas as pl
from jax.experimental.pallas import tpu as pltpu
from jax.sharding import PartitionSpec as P

ITERS = 2
ROOTS = 2
NX = 4
ORDER = "01010101010101010101010101010101"
MESH = pl.DeviceIdType.MESH
F32 = jnp.float32
BF16 = jnp.bfloat16


def dot(a, b):
    return jnp.dot(a, b, preferred_element_type=F32)


def dot_nt(a, b):
    return lax.dot_general(a, b, (((1,), (1,)), ((), ())), preferred_element_type=F32)


def remote(src, dst, send, recv, device):
    return pltpu.make_async_remote_copy(
        src_ref=src, dst_ref=dst, send_sem=send, recv_sem=recv, device_id=device, device_id_type=MESH
    )


def kernel(
    ns, nz, wave, diagonal, left_hbm, right_hbm, offsets, out,
    left, right, perm, first, keep, cross, halves, pieces, rows, stay, cross_out, cross_in,
    far_out, far_in, near_out, near_in, share_out, share_in, chunk_buf,
    load_sem, gz_s, gz_r, gx_s, gx_r, y_s, y_r, xa_s, xa_r, xb_s, xb_r, z_s, z_r,
):
    npairs, size = left.shape[0], left.shape[1]
    chunk = size // NX
    half = chunk // 2
    piece = chunk // nz

    s = lax.axis_index("sec")
    o = lax.axis_index("op")
    z = o // NX
    x = o % NX
    right_x, left_x, far_x = (x + 1) % NX, (x + NX - 1) % NX, (x + 2) % NX
    around = (x, right_x, far_x, left_x)
    x_devs = ((s, z * NX + right_x), (s, z * NX + left_x))
    has_up, has_down = s < ns - 1, s > 0
    up_dev, down_dev = (s + 1, o), (s - 1, o)

    def z_peer(d):
        return (z + d) % nz

    def z_dev(d):
        return (s, z_peer(d) * NX + x)

    load_l = pltpu.make_async_copy(left_hbm, left, load_sem.at[0])
    load_r = pltpu.make_async_copy(right_hbm, right, load_sem.at[1])
    load_l.start()
    load_r.start()

    for r in range(ROOTS):
        pieces[0, r, z] = wave[0].astype(F32)[:, r, :].astype(BF16)

    barrier = pltpu.get_barrier_semaphore()
    for d in range(1, nz):
        pl.semaphore_signal(barrier, inc=1, device_id=z_dev(d), device_id_type=MESH)
    pl.semaphore_signal(barrier, inc=1, device_id=x_devs[0], device_id_type=MESH)
    pl.semaphore_signal(barrier, inc=1, device_id=x_devs[1], device_id_type=MESH)

    for other in ((s + 1) % ns, (s + ns - 1) % ns):
        pl.semaphore_signal(barrier, inc=1, device_id=(other, o), device_id_type=MESH)
    pl.semaphore_wait(barrier, nz + 3)

    order = sorted(range(1, nz), key=lambda d: -min(d, nz - d))

    def gz(it, r, d):
        mine, theirs = pieces.at[it, r, z], pieces.at[it, r, z_peer(nz - d)]
        return mine, mine, theirs, gz_s.at[it, r, d - 1], gz_r.at[it, r, d - 1], z_dev(d), None, None

    def gx(it, r, way):
        mine, theirs = rows.at[it, r, x], rows.at[it, r, left_x if way == 0 else right_x]
        return mine, mine, theirs, gx_s.at[it, r, way], gx_r.at[it, r, way], x_devs[way], None, None

    def gf(it, r, way):
        part = pl.ds(half * way, half)
        mine, theirs = rows.at[it, r, left_x if way == 0 else right_x, part], rows.at[it, r, far_x, part]
        return mine, mine, theirs, gx_s.at[it, r, 2 + way], gx_r.at[it, r, 2 + way], x_devs[way], None, None

    def yy(it, r, way, j):
        q = around[j]
        there = cross_in.at[it, r, way, q]
        device, leaves, comes = (up_dev, has_up, has_down) if way == 0 else (down_dev, has_down, has_up)
        return (
            cross_out.at[it, r, way, q], there, there,
            y_s.at[it, r, way, j], y_r.at[it, r, way, j], device, leaves, comes,
        )

    def xa(it, r, way):
        there = far_in.at[it, r, way]
        return far_out.at[it, r, way], there, there, xa_s.at[it, r, way], xa_r.at[it, r, way], x_devs[way], None, None

    def xb(it, r, way):
        there = near_in.at[it, r, way]
        return near_out.at[it, r, way], there, there, xb_s.at[it, r, way], xb_r.at[it, r, way], x_devs[way], None, None

    def zz(it, r, d):
        return (
            share_out.at[it, r, z_peer(d)], share_in.at[it, r, z], share_in.at[it, r, z_peer(nz - d)],
            z_s.at[it, r, d - 1], z_r.at[it, r, d - 1], z_dev(d), None, None,
        )

    def act(condition, action):
        if condition is None:
            action()
        else:
            pl.when(condition)(action)

    started, received = [], set()

    def send(kind, *key):
        src, dst, _, send_sem, recv_sem, device, leaves, _ = kind(*key)
        act(leaves, lambda: remote(src, dst, send_sem, recv_sem, device).start())
        started.append((kind, key))

    def sent(kind, *key):
        src, dst, _, send_sem, recv_sem, device, leaves, _ = kind(*key)
        act(leaves, lambda: remote(src, dst, send_sem, recv_sem, device).wait_send())

    def recv(kind, *key):
        src, _, dst, send_sem, recv_sem, device, _, comes = kind(*key)
        act(comes, lambda: remote(src, dst, send_sem, recv_sem, device).wait_recv())
        received.add((kind, key))

    def gather_z_send(it, r):
        for d in order:
            send(gz, it, r, d)

    def gather_x_send(it, r):
        for d in reversed(order):
            recv(gz, it, r, d)
        for k in range(nz):
            chunk_buf[piece * k : piece * (k + 1), :] = pieces[it, r, k].astype(F32)
        rows[it, r, x] = chunk_buf[...].astype(BF16)
        send(gx, it, r, 0)
        send(gx, it, r, 1)

    def gather_x_forward(it, r):
        for way in range(2):
            recv(gx, it, r, way)
            send(gf, it, r, way)

    def prepare():
        shape = (size, size)
        position = lax.broadcasted_iota(jnp.int32, shape, 0)
        column = lax.broadcasted_iota(jnp.int32, shape, 1)
        x_part = jnp.zeros(shape, jnp.int32)
        for k in range(1, NX):
            x_part = x_part + jnp.where(position >= chunk * k, 1, 0)
        inside = position - chunk * x_part
        z_part = jnp.zeros(shape, jnp.int32)
        for k in range(1, nz):
            z_part = z_part + jnp.where(inside >= piece * k, 1, 0)
        source = (inside - piece * z_part) + piece * x_part + (NX * piece) * z_part
        perm[...] = jnp.where(source == column, 1.0, 0.0).astype(BF16)
        perm_eye = jnp.where(position == column, 1.0, 0.0).astype(BF16)
        load_r.wait()
        for p in range(npairs):
            cols = slice(size * p, size * (p + 1))
            first[0, :, cols] = dot_nt(perm_eye, right[p]).astype(BF16)
            first[1, :, cols] = right[p]
        load_l.wait()
        for p in range(npairs):
            up = offsets[0, p].astype(F32)
            down = offsets[1, p].astype(F32)
            turned_rows = dot(perm[...], left[p]).astype(BF16)
            direct = dot_nt(turned_rows, perm[...])
            cols = slice(size * p, size * (p + 1))
            more = slice(size * (npairs + p), size * (npairs + p + 1))
            keep[:, cols] = (direct * (1.0 - up)).astype(BF16)
            cross[0, :, cols] = (direct * up).astype(BF16)
            transposed = dot_nt(perm[...], turned_rows)
            keep[:, more] = (transposed * (1.0 - down)).astype(BF16)
            cross[1, :, cols] = (transposed * down).astype(BF16)

        blank = jnp.zeros((NX, chunk, size), BF16)

        @pl.when(s == 0)
        def _():
            for it in range(ITERS):
                for r in range(ROOTS):
                    cross_in[it, r, 0] = blank

        @pl.when(s == ns - 1)
        def _():
            for it in range(ITERS):
                for r in range(ROOTS):
                    cross_in[it, r, 1] = blank

    def compute_cross(it, r):
        recv(gf, it, r, 0)
        recv(gf, it, r, 1)
        vector = rows[it, r].reshape(size, size)

        def stage_one(i, carry):
            product = dot(vector, first[i]).astype(BF16)
            for p in range(npairs):
                halves[r, i, p] = product[:, size * p : size * (p + 1)]
            return carry

        lax.fori_loop(0, 2, stage_one, 0)
        for way in range(2):
            half_sum = dot(cross[way], halves[r, way].reshape(npairs * size, size))
            cross_out[it, r, way] = half_sum.astype(BF16).reshape(NX, chunk, size)
            for j in (2, 1, 3, 0):
                send(yy, it, r, way, j)

    def compute_own(it, r):
        own = dot(keep[...], halves[r].reshape(2 * npairs * size, size))
        stay[r] = own.reshape(NX, chunk, size)

    def total(it, r, j):
        recv(yy, it, r, 0, j)
        recv(yy, it, r, 1, j)
        q = around[j]
        return stay[r, q] + cross_in[it, r, 0, q].astype(F32) + cross_in[it, r, 1, q].astype(F32)

    def reduce_x_far(it, r):
        block = total(it, r, 2)
        far_out[it, r, 0] = block[:half].astype(BF16)
        far_out[it, r, 1] = block[half:].astype(BF16)
        send(xa, it, r, 0)
        send(xa, it, r, 1)

    def reduce_x_near(it, r):
        block = total(it, r, 1)
        near_out[it, r, 0, half:] = block[half:].astype(BF16)
        recv(xa, it, r, 0)
        near_out[it, r, 0, :half] = (block[:half] + far_in[it, r, 0].astype(F32)).astype(BF16)
        send(xb, it, r, 0)
        block = total(it, r, 3)
        near_out[it, r, 1, :half] = block[:half].astype(BF16)
        recv(xa, it, r, 1)
        near_out[it, r, 1, half:] = (block[half:] + far_in[it, r, 1].astype(F32)).astype(BF16)
        send(xb, it, r, 1)
        stay[r, x] = total(it, r, 0)

    def reduce_z_send(it, r):
        recv(xb, it, r, 0)
        recv(xb, it, r, 1)
        chunk_buf[...] = stay[r, x] + near_in[it, r, 0].astype(F32) + near_in[it, r, 1].astype(F32)
        for k in range(nz):
            share_out[it, r, k] = chunk_buf[piece * k : piece * (k + 1), :].astype(BF16)
        for d in order:
            send(zz, it, r, d)
        share_in[it, r, z] = share_out[it, r, z]

    def finish(it, r):
        for d in reversed(order):
            recv(zz, it, r, d)
        sigma = share_in[it, r, 0].astype(F32)
        for k in range(1, nz):
            sigma = sigma + share_in[it, r, k].astype(F32)
        result = sigma / diagonal[:, 0, :]
        if it < ITERS - 1:
            pieces[it + 1, r, z] = result.astype(BF16)
            gather_z_send(it + 1, r)
        else:
            results.append(result)

    steps = [functools.partial(gather_z_send, 0, r) for r in range(ROOTS)] + [prepare]
    queues = [[], []]
    for it in range(ITERS):
        for step in (
            gather_x_send, gather_x_forward, compute_cross, compute_own,
            reduce_x_far, reduce_x_near, reduce_z_send, finish,
        ):
            for r in range(ROOTS):
                queues[r].append(functools.partial(step, it, r))
    for r in ORDER:
        steps.append(queues[int(r)].pop(0))
    results = []
    for step in steps:
        step()
    out[0] = jnp.stack(results, axis=1).astype(BF16)
    for kind, key in started:
        sent(kind, *key)


def on_device(ns, nz, wavefunction, diagonal, left_ops, right_ops, offsets):
    npairs, size, _ = left_ops.shape
    chunk = size // NX
    half = chunk // 2
    piece = chunk // nz
    it2 = (ITERS, ROOTS)
    dma = pltpu.SemaphoreType.DMA
    vmem = pl.BlockSpec(memory_space=pltpu.VMEM)
    result = pl.pallas_call(
        functools.partial(kernel, ns, nz),
        out_shape=jax.ShapeDtypeStruct((1, piece, ROOTS, size), BF16),
        in_specs=[
            vmem, vmem, pl.BlockSpec(memory_space=pl.ANY), pl.BlockSpec(memory_space=pl.ANY),
            pl.BlockSpec(memory_space=pltpu.SMEM),
        ],
        out_specs=vmem,
        scratch_shapes=[
            pltpu.VMEM((npairs, size, size), BF16),
            pltpu.VMEM((npairs, size, size), BF16),
            pltpu.VMEM((size, size), BF16),
            pltpu.VMEM((2, size, npairs * size), BF16),
            pltpu.VMEM((size, 2 * npairs * size), BF16),
            pltpu.VMEM((2, size, npairs * size), BF16),
            pltpu.VMEM((ROOTS, 2, npairs, size, size), BF16),
            pltpu.VMEM(it2 + (nz, piece, size), BF16),
            pltpu.VMEM(it2 + (NX, chunk, size), BF16),
            pltpu.VMEM((ROOTS, NX, chunk, size), F32),
            pltpu.VMEM(it2 + (2, NX, chunk, size), BF16),
            pltpu.VMEM(it2 + (2, NX, chunk, size), BF16),
            pltpu.VMEM(it2 + (2, half, size), BF16),
            pltpu.VMEM(it2 + (2, half, size), BF16),
            pltpu.VMEM(it2 + (2, chunk, size), BF16),
            pltpu.VMEM(it2 + (2, chunk, size), BF16),
            pltpu.VMEM(it2 + (nz, piece, size), BF16),
            pltpu.VMEM(it2 + (nz, piece, size), BF16),
            pltpu.VMEM((chunk, size), F32),
            dma((2,)),
            dma(it2 + (nz - 1,)), dma(it2 + (nz - 1,)),
            dma(it2 + (4,)), dma(it2 + (4,)),
            dma(it2 + (2, NX)), dma(it2 + (2, NX)),
            dma(it2 + (2,)), dma(it2 + (2,)),
            dma(it2 + (2,)), dma(it2 + (2,)),
            dma(it2 + (nz - 1,)), dma(it2 + (nz - 1,)),
        ],
        compiler_params=pltpu.CompilerParams(
            collective_id=0, has_side_effects=True, vmem_limit_bytes=60000 * 1024
        ),
        name="sigma_twice",
    )(
        wavefunction.transpose(0, 2, 1, 3), diagonal.transpose(1, 0, 2), left_ops, right_ops, offsets.T
    )
    return result.transpose(0, 2, 1, 3)


def solution(mesh):
    in_specs = (
        P("sec", None, "op", None),
        P("sec", "op", None),
        P(("sec", "op"), None, None),
        P(("sec", "op"), None, None),
        P(("sec", "op"), None),
    )
    out_specs = P("sec", None, "op", None)
    body = functools.partial(on_device, mesh.shape["sec"], mesh.shape["op"] // NX)
    return jax.shard_map(
        body, mesh=mesh, in_specs=in_specs, out_specs=out_specs, check_vma=False
    )
```

```python
import functools

import jax
import jax.numpy as jnp
from jax import lax
from jax.experimental import pallas as pl
from jax.experimental.pallas import tpu as pltpu
from jax.sharding import PartitionSpec as P

ITERS = 2
ROOTS = 2
NX = 4
ORDER = "010101010101010101010101"
MESH = pl.DeviceIdType.MESH
F32 = jnp.float32
BF16 = jnp.bfloat16


def dot(a, b):
    return jnp.dot(a, b, preferred_element_type=F32)


def dot_nt(a, b):
    return lax.dot_general(a, b, (((1,), (1,)), ((), ())), preferred_element_type=F32)


def remote(src, dst, send, recv, device):
    return pltpu.make_async_remote_copy(
        src_ref=src, dst_ref=dst, send_sem=send, recv_sem=recv, device_id=device, device_id_type=MESH
    )


def kernel(
    ns, nz, wave, diagonal, left_hbm, right_hbm, offsets, out,
    left, right, perm, first, keep, cross, halves, pieces, rows, stay, cross_out, cross_in,
    near_out, near_in, share_out, share_in, chunk_buf,
    load_sem, gz_s, gz_r, gx_s, gx_r, y_s, y_r, xx_s, xx_r, z_s, z_r,
):
    npairs, size = left.shape[0], left.shape[1]
    chunk = size // NX
    piece = chunk // nz

    s = lax.axis_index("sec")
    o = lax.axis_index("op")
    z = o // NX
    x = o % NX
    around = tuple((x + j) % NX for j in range(NX))
    has_up, has_down = s < ns - 1, s > 0
    up_dev, down_dev = (s + 1, o), (s - 1, o)

    def z_peer(d):
        return (z + d) % nz

    def x_dev(j):
        return (s, z * NX + around[j])

    def z_dev(d):
        return (s, z_peer(d) * NX + x)

    load_l = pltpu.make_async_copy(left_hbm, left, load_sem.at[0])
    load_r = pltpu.make_async_copy(right_hbm, right, load_sem.at[1])
    load_l.start()
    load_r.start()

    for r in range(ROOTS):
        pieces[0, r, z] = wave[0].astype(F32)[:, r, :].astype(BF16)

    barrier = pltpu.get_barrier_semaphore()
    for d in range(1, nz):
        pl.semaphore_signal(barrier, inc=1, device_id=z_dev(d), device_id_type=MESH)
    for j in range(1, NX):
        pl.semaphore_signal(barrier, inc=1, device_id=x_dev(j), device_id_type=MESH)
    for other in ((s + 1) % ns, (s + ns - 1) % ns):
        pl.semaphore_signal(barrier, inc=1, device_id=(other, o), device_id_type=MESH)
    pl.semaphore_wait(barrier, nz + NX)

    x_order = sorted(range(1, NX), key=lambda j: -min(j, NX - j))
    order = sorted(range(1, nz), key=lambda d: -min(d, nz - d))

    def gz(it, r, d):
        mine, theirs = pieces.at[it, r, z], pieces.at[it, r, z_peer(nz - d)]
        return mine, mine, theirs, gz_s.at[it, r, d - 1], gz_r.at[it, r, d - 1], z_dev(d), None, None

    def gx(it, r, j):
        mine, theirs = rows.at[it, r, x], rows.at[it, r, around[NX - j]]
        return mine, mine, theirs, gx_s.at[it, r, j - 1], gx_r.at[it, r, j - 1], x_dev(j), None, None

    def yy(it, r, way, j):
        q = around[j]
        there = cross_in.at[it, r, way, q]
        device, leaves, comes = (up_dev, has_up, has_down) if way == 0 else (down_dev, has_down, has_up)
        return (
            cross_out.at[it, r, way, q], there, there,
            y_s.at[it, r, way, j], y_r.at[it, r, way, j], device, leaves, comes,
        )

    def xx(it, r, j):
        there = near_in.at[it, r, j - 1]
        return near_out.at[it, r, j - 1], there, there, xx_s.at[it, r, j - 1], xx_r.at[it, r, j - 1], x_dev(j), None, None

    def zz(it, r, d):
        return (
            share_out.at[it, r, z_peer(d)], share_in.at[it, r, z], share_in.at[it, r, z_peer(nz - d)],
            z_s.at[it, r, d - 1], z_r.at[it, r, d - 1], z_dev(d), None, None,
        )

    def act(condition, action):
        if condition is None:
            action()
        else:
            pl.when(condition)(action)

    started, received = [], set()

    def send(kind, *key):
        src, dst, _, send_sem, recv_sem, device, leaves, _ = kind(*key)
        act(leaves, lambda: remote(src, dst, send_sem, recv_sem, device).start())
        started.append((kind, key))

    def sent(kind, *key):
        src, dst, _, send_sem, recv_sem, device, leaves, _ = kind(*key)
        act(leaves, lambda: remote(src, dst, send_sem, recv_sem, device).wait_send())

    def recv(kind, *key):
        src, _, dst, send_sem, recv_sem, device, _, comes = kind(*key)
        act(comes, lambda: remote(src, dst, send_sem, recv_sem, device).wait_recv())
        received.add((kind, key))

    def gather_z_send(it, r):
        for d in order:
            send(gz, it, r, d)

    def gather_x_send(it, r):
        for d in reversed(order):
            recv(gz, it, r, d)
        for k in range(nz):
            chunk_buf[piece * k : piece * (k + 1), :] = pieces[it, r, k].astype(F32)
        rows[it, r, x] = chunk_buf[...].astype(BF16)
        for j in x_order:
            send(gx, it, r, j)

    def prepare():
        shape = (size, size)
        position = lax.broadcasted_iota(jnp.int32, shape, 0)
        column = lax.broadcasted_iota(jnp.int32, shape, 1)
        x_part = jnp.zeros(shape, jnp.int32)
        for k in range(1, NX):
            x_part = x_part + jnp.where(position >= chunk * k, 1, 0)
        inside = position - chunk * x_part
        z_part = jnp.zeros(shape, jnp.int32)
        for k in range(1, nz):
            z_part = z_part + jnp.where(inside >= piece * k, 1, 0)
        source = (inside - piece * z_part) + piece * x_part + (NX * piece) * z_part
        perm[...] = jnp.where(source == column, 1.0, 0.0).astype(BF16)
        perm_eye = jnp.where(position == column, 1.0, 0.0).astype(BF16)
        load_r.wait()
        for p in range(npairs):
            cols = slice(size * p, size * (p + 1))
            first[0, :, cols] = dot_nt(perm_eye, right[p]).astype(BF16)
            first[1, :, cols] = right[p]
        load_l.wait()
        for p in range(npairs):
            up = offsets[0, p].astype(F32)
            down = offsets[1, p].astype(F32)
            turned_rows = dot(perm[...], left[p]).astype(BF16)
            direct = dot_nt(turned_rows, perm[...])
            cols = slice(size * p, size * (p + 1))
            more = slice(size * (npairs + p), size * (npairs + p + 1))
            keep[:, cols] = (direct * (1.0 - up)).astype(BF16)
            cross[0, :, cols] = (direct * up).astype(BF16)
            transposed = dot_nt(perm[...], turned_rows)
            keep[:, more] = (transposed * (1.0 - down)).astype(BF16)
            cross[1, :, cols] = (transposed * down).astype(BF16)

        blank = jnp.zeros((NX, chunk, size), BF16)

        @pl.when(s == 0)
        def _():
            for it in range(ITERS):
                for r in range(ROOTS):
                    cross_in[it, r, 0] = blank

        @pl.when(s == ns - 1)
        def _():
            for it in range(ITERS):
                for r in range(ROOTS):
                    cross_in[it, r, 1] = blank

    def compute_cross(it, r):
        for j in reversed(x_order):
            recv(gx, it, r, j)
        vector = rows[it, r].reshape(size, size)

        def stage_one(i, carry):
            product = dot(vector, first[i]).astype(BF16)
            for p in range(npairs):
                halves[r, i, p] = product[:, size * p : size * (p + 1)]
            return carry

        lax.fori_loop(0, 2, stage_one, 0)
        for way in range(2):
            half_sum = dot(cross[way], halves[r, way].reshape(npairs * size, size))
            cross_out[it, r, way] = half_sum.astype(BF16).reshape(NX, chunk, size)
            for j in x_order + [0]:
                send(yy, it, r, way, j)

    def compute_own(it, r):
        own = dot(keep[...], halves[r].reshape(2 * npairs * size, size))
        stay[r] = own.reshape(NX, chunk, size)

    def total(it, r, j):
        recv(yy, it, r, 0, j)
        recv(yy, it, r, 1, j)
        q = around[j]
        return stay[r, q] + cross_in[it, r, 0, q].astype(F32) + cross_in[it, r, 1, q].astype(F32)

    def reduce_x_send(it, r):
        for j in x_order:
            near_out[it, r, j - 1] = total(it, r, j).astype(BF16)
            send(xx, it, r, j)
        stay[r, x] = total(it, r, 0)

    def reduce_z_send(it, r):
        block = stay[r, x]
        for j in reversed(x_order):
            recv(xx, it, r, j)
            block = block + near_in[it, r, j - 1].astype(F32)
        chunk_buf[...] = block
        for k in range(nz):
            share_out[it, r, k] = chunk_buf[piece * k : piece * (k + 1), :].astype(BF16)
        for d in order:
            send(zz, it, r, d)
        share_in[it, r, z] = share_out[it, r, z]

    def finish(it, r):
        for d in reversed(order):
            recv(zz, it, r, d)
        sigma = share_in[it, r, 0].astype(F32)
        for k in range(1, nz):
            sigma = sigma + share_in[it, r, k].astype(F32)
        result = sigma / diagonal[:, 0, :]
        if it < ITERS - 1:
            pieces[it + 1, r, z] = result.astype(BF16)
            gather_z_send(it + 1, r)
        else:
            results.append(result)

    steps = [functools.partial(gather_z_send, 0, r) for r in range(ROOTS)] + [prepare]
    queues = [[], []]
    for it in range(ITERS):
        for step in (
            gather_x_send, compute_cross, compute_own, reduce_x_send, reduce_z_send, finish
        ):
            for r in range(ROOTS):
                queues[r].append(functools.partial(step, it, r))
    for r in ORDER:
        steps.append(queues[int(r)].pop(0))
    results = []
    for step in steps:
        step()
    out[0] = jnp.stack(results, axis=1).astype(BF16)
    for kind, key in started:
        sent(kind, *key)


def on_device(ns, nz, wavefunction, diagonal, left_ops, right_ops, offsets):
    npairs, size, _ = left_ops.shape
    chunk = size // NX
    piece = chunk // nz
    it2 = (ITERS, ROOTS)
    dma = pltpu.SemaphoreType.DMA
    vmem = pl.BlockSpec(memory_space=pltpu.VMEM)
    result = pl.pallas_call(
        functools.partial(kernel, ns, nz),
        out_shape=jax.ShapeDtypeStruct((1, piece, ROOTS, size), BF16),
        in_specs=[
            vmem, vmem, pl.BlockSpec(memory_space=pl.ANY), pl.BlockSpec(memory_space=pl.ANY),
            pl.BlockSpec(memory_space=pltpu.SMEM),
        ],
        out_specs=vmem,
        scratch_shapes=[
            pltpu.VMEM((npairs, size, size), BF16),
            pltpu.VMEM((npairs, size, size), BF16),
            pltpu.VMEM((size, size), BF16),
            pltpu.VMEM((2, size, npairs * size), BF16),
            pltpu.VMEM((size, 2 * npairs * size), BF16),
            pltpu.VMEM((2, size, npairs * size), BF16),
            pltpu.VMEM((ROOTS, 2, npairs, size, size), BF16),
            pltpu.VMEM(it2 + (nz, piece, size), BF16),
            pltpu.VMEM(it2 + (NX, chunk, size), BF16),
            pltpu.VMEM((ROOTS, NX, chunk, size), F32),
            pltpu.VMEM(it2 + (2, NX, chunk, size), BF16),
            pltpu.VMEM(it2 + (2, NX, chunk, size), BF16),
            pltpu.VMEM(it2 + (NX - 1, chunk, size), BF16),
            pltpu.VMEM(it2 + (NX - 1, chunk, size), BF16),
            pltpu.VMEM(it2 + (nz, piece, size), BF16),
            pltpu.VMEM(it2 + (nz, piece, size), BF16),
            pltpu.VMEM((chunk, size), F32),
            dma((2,)),
            dma(it2 + (nz - 1,)), dma(it2 + (nz - 1,)),
            dma(it2 + (NX - 1,)), dma(it2 + (NX - 1,)),
            dma(it2 + (2, NX)), dma(it2 + (2, NX)),
            dma(it2 + (NX - 1,)), dma(it2 + (NX - 1,)),
            dma(it2 + (nz - 1,)), dma(it2 + (nz - 1,)),
        ],
        compiler_params=pltpu.CompilerParams(
            collective_id=0, has_side_effects=True, vmem_limit_bytes=60000 * 1024
        ),
        name="sigma_twice",
    )(
        wavefunction.transpose(0, 2, 1, 3), diagonal.transpose(1, 0, 2), left_ops, right_ops, offsets.T
    )
    return result.transpose(0, 2, 1, 3)


def solution(mesh):
    in_specs = (
        P("sec", None, "op", None),
        P("sec", "op", None),
        P(("sec", "op"), None, None),
        P(("sec", "op"), None, None),
        P(("sec", "op"), None),
    )
    out_specs = P("sec", None, "op", None)
    body = functools.partial(on_device, mesh.shape["sec"], mesh.shape["op"] // NX)
    return jax.shard_map(
        body, mesh=mesh, in_specs=in_specs, out_specs=out_specs, check_vma=False
    )
```

```python
import functools

import jax
import jax.numpy as jnp
from jax import lax
from jax.experimental import pallas as pl
from jax.experimental.pallas import tpu as pltpu
from jax.sharding import PartitionSpec as P

ITERS = 2
ROOTS = 2
NX = 4
ORDER = "010100110101010100110101"
MESH = pl.DeviceIdType.MESH
F32 = jnp.float32
BF16 = jnp.bfloat16


def dot(a, b):
    return jnp.dot(a, b, preferred_element_type=F32)


def dot_nt(a, b):
    return lax.dot_general(a, b, (((1,), (1,)), ((), ())), preferred_element_type=F32)


def remote(src, dst, send, recv, device):
    return pltpu.make_async_remote_copy(
        src_ref=src, dst_ref=dst, send_sem=send, recv_sem=recv, device_id=device, device_id_type=MESH
    )


def kernel(
    ns, nz, wave, diagonal, left_hbm, right_hbm, offsets, out,
    left, right, perm, first, keep, cross, halves, pieces, rows, stay, cross_out, cross_in,
    near_out, near_in, share_out, share_in, chunk_buf,
    load_sem, gz_s, gz_r, gx_s, gx_r, y_s, y_r, xx_s, xx_r, z_s, z_r,
):
    npairs, size = left.shape[0], left.shape[1]
    chunk = size // NX
    piece = chunk // nz

    s = lax.axis_index("sec")
    o = lax.axis_index("op")
    z = o // NX
    x = o % NX
    around = tuple((x + j) % NX for j in range(NX))
    has_up, has_down = s < ns - 1, s > 0
    up_dev, down_dev = (s + 1, o), (s - 1, o)

    def z_peer(d):
        return (z + d) % nz

    def x_dev(j):
        return (s, z * NX + around[j])

    def z_dev(d):
        return (s, z_peer(d) * NX + x)

    load_l = pltpu.make_async_copy(left_hbm, left, load_sem.at[0])
    load_r = pltpu.make_async_copy(right_hbm, right, load_sem.at[1])
    load_l.start()
    load_r.start()

    for r in range(ROOTS):
        pieces[0, r, z] = wave[0].astype(F32)[:, r, :].astype(BF16)

    barrier = pltpu.get_barrier_semaphore()
    for d in range(1, nz):
        pl.semaphore_signal(barrier, inc=1, device_id=z_dev(d), device_id_type=MESH)
    for j in range(1, NX):
        pl.semaphore_signal(barrier, inc=1, device_id=x_dev(j), device_id_type=MESH)
    for other in ((s + 1) % ns, (s + ns - 1) % ns):
        pl.semaphore_signal(barrier, inc=1, device_id=(other, o), device_id_type=MESH)
    pl.semaphore_wait(barrier, nz + NX)

    x_order = sorted(range(1, NX), key=lambda j: -min(j, NX - j))
    order = sorted(range(1, nz), key=lambda d: -min(d, nz - d))

    def gz(it, r, d):
        mine, theirs = pieces.at[it, r, z], pieces.at[it, r, z_peer(nz - d)]
        return mine, mine, theirs, gz_s.at[it, r, d - 1], gz_r.at[it, r, d - 1], z_dev(d), None, None

    def gx(it, r, j):
        mine, theirs = rows.at[it, r, x], rows.at[it, r, around[NX - j]]
        return mine, mine, theirs, gx_s.at[it, r, j - 1], gx_r.at[it, r, j - 1], x_dev(j), None, None

    def yy(it, r, way, j):
        q = around[j]
        there = cross_in.at[it, r, way, q]
        device, leaves, comes = (up_dev, has_up, has_down) if way == 0 else (down_dev, has_down, has_up)
        return (
            cross_out.at[it, r, way, q], there, there,
            y_s.at[it, r, way, j], y_r.at[it, r, way, j], device, leaves, comes,
        )

    def xx(it, r, j):
        there = near_in.at[it, r, j - 1]
        return near_out.at[it, r, j - 1], there, there, xx_s.at[it, r, j - 1], xx_r.at[it, r, j - 1], x_dev(j), None, None

    def zz(it, r, d):
        return (
            share_out.at[it, r, z_peer(d)], share_in.at[it, r, z], share_in.at[it, r, z_peer(nz - d)],
            z_s.at[it, r, d - 1], z_r.at[it, r, d - 1], z_dev(d), None, None,
        )

    def act(condition, action):
        if condition is None:
            action()
        else:
            pl.when(condition)(action)

    started, received = [], set()

    def send(kind, *key):
        src, dst, _, send_sem, recv_sem, device, leaves, _ = kind(*key)
        act(leaves, lambda: remote(src, dst, send_sem, recv_sem, device).start())
        started.append((kind, key))

    def sent(kind, *key):
        src, dst, _, send_sem, recv_sem, device, leaves, _ = kind(*key)
        act(leaves, lambda: remote(src, dst, send_sem, recv_sem, device).wait_send())

    def recv(kind, *key):
        src, _, dst, send_sem, recv_sem, device, _, comes = kind(*key)
        act(comes, lambda: remote(src, dst, send_sem, recv_sem, device).wait_recv())
        received.add((kind, key))

    def gather_z_send(it, r):
        for d in order:
            send(gz, it, r, d)

    def gather_x_send(it, r):
        for d in reversed(order):
            recv(gz, it, r, d)
        for k in range(nz):
            chunk_buf[piece * k : piece * (k + 1), :] = pieces[it, r, k].astype(F32)
        rows[it, r, x] = chunk_buf[...].astype(BF16)
        for j in x_order:
            send(gx, it, r, j)

    def prepare():
        shape = (size, size)
        position = lax.broadcasted_iota(jnp.int32, shape, 0)
        column = lax.broadcasted_iota(jnp.int32, shape, 1)
        x_part = jnp.zeros(shape, jnp.int32)
        for k in range(1, NX):
            x_part = x_part + jnp.where(position >= chunk * k, 1, 0)
        inside = position - chunk * x_part
        z_part = jnp.zeros(shape, jnp.int32)
        for k in range(1, nz):
            z_part = z_part + jnp.where(inside >= piece * k, 1, 0)
        source = (inside - piece * z_part) + piece * x_part + (NX * piece) * z_part
        perm[...] = jnp.where(source == column, 1.0, 0.0).astype(BF16)
        perm_eye = jnp.where(position == column, 1.0, 0.0).astype(BF16)
        load_r.wait()
        for p in range(npairs):
            cols = slice(size * p, size * (p + 1))
            first[0, :, cols] = dot_nt(perm_eye, right[p]).astype(BF16)
            first[1, :, cols] = right[p]
        load_l.wait()
        for p in range(npairs):
            up = offsets[0, p].astype(F32)
            down = offsets[1, p].astype(F32)
            turned_rows = dot(perm[...], left[p]).astype(BF16)
            direct = dot_nt(turned_rows, perm[...])
            cols = slice(size * p, size * (p + 1))
            more = slice(size * (npairs + p), size * (npairs + p + 1))
            keep[:, cols] = (direct * (1.0 - up)).astype(BF16)
            cross[0, :, cols] = (direct * up).astype(BF16)
            transposed = dot_nt(perm[...], turned_rows)
            keep[:, more] = (transposed * (1.0 - down)).astype(BF16)
            cross[1, :, cols] = (transposed * down).astype(BF16)

        blank = jnp.zeros((NX, chunk, size), BF16)

        @pl.when(s == 0)
        def _():
            for it in range(ITERS):
                for r in range(ROOTS):
                    cross_in[it, r, 0] = blank

        @pl.when(s == ns - 1)
        def _():
            for it in range(ITERS):
                for r in range(ROOTS):
                    cross_in[it, r, 1] = blank

    def compute_cross(it, r):
        for j in reversed(x_order):
            recv(gx, it, r, j)
        vector = rows[it, r].reshape(size, size)

        for way in range(2):
            product = dot(vector, first[way]).astype(BF16)
            for p in range(npairs):
                halves[r, way, p] = product[:, size * p : size * (p + 1)]
            half_sum = dot(cross[way], halves[r, way].reshape(npairs * size, size))
            cross_out[it, r, way] = half_sum.astype(BF16).reshape(NX, chunk, size)
            for j in x_order + [0]:
                send(yy, it, r, way, j)

    def compute_own(it, r):
        own = dot(keep[...], halves[r].reshape(2 * npairs * size, size))
        stay[r] = own.reshape(NX, chunk, size)

    def total(it, r, j):
        recv(yy, it, r, 0, j)
        recv(yy, it, r, 1, j)
        q = around[j]
        return stay[r, q] + cross_in[it, r, 0, q].astype(F32) + cross_in[it, r, 1, q].astype(F32)

    def reduce_x_send(it, r):
        for j in x_order:
            near_out[it, r, j - 1] = total(it, r, j).astype(BF16)
            send(xx, it, r, j)
        stay[r, x] = total(it, r, 0)

    def reduce_z_send(it, r):
        block = stay[r, x]
        for j in reversed(x_order):
            recv(xx, it, r, j)
            block = block + near_in[it, r, j - 1].astype(F32)
        chunk_buf[...] = block
        for k in range(nz):
            share_out[it, r, k] = chunk_buf[piece * k : piece * (k + 1), :].astype(BF16)
        for d in order:
            send(zz, it, r, d)
        share_in[it, r, z] = share_out[it, r, z]

    def finish(it, r):
        for d in reversed(order):
            recv(zz, it, r, d)
        sigma = share_in[it, r, 0].astype(F32)
        for k in range(1, nz):
            sigma = sigma + share_in[it, r, k].astype(F32)
        result = sigma / diagonal[:, 0, :]
        if it < ITERS - 1:
            pieces[it + 1, r, z] = result.astype(BF16)
            gather_z_send(it + 1, r)
        else:
            results.append(result)

    steps = [functools.partial(gather_z_send, 0, r) for r in range(ROOTS)] + [prepare]
    queues = [[], []]
    for it in range(ITERS):
        for step in (
            gather_x_send, compute_cross, compute_own, reduce_x_send, reduce_z_send, finish
        ):
            for r in range(ROOTS):
                queues[r].append(functools.partial(step, it, r))
    for r in ORDER:
        steps.append(queues[int(r)].pop(0))
    results = []
    for step in steps:
        step()
    out[0] = jnp.stack(results, axis=1).astype(BF16)
    for kind, key in started:
        sent(kind, *key)


def on_device(ns, nz, wavefunction, diagonal, left_ops, right_ops, offsets):
    npairs, size, _ = left_ops.shape
    chunk = size // NX
    piece = chunk // nz
    it2 = (ITERS, ROOTS)
    dma = pltpu.SemaphoreType.DMA
    vmem = pl.BlockSpec(memory_space=pltpu.VMEM)
    result = pl.pallas_call(
        functools.partial(kernel, ns, nz),
        out_shape=jax.ShapeDtypeStruct((1, piece, ROOTS, size), BF16),
        in_specs=[
            vmem, vmem, pl.BlockSpec(memory_space=pl.ANY), pl.BlockSpec(memory_space=pl.ANY),
            pl.BlockSpec(memory_space=pltpu.SMEM),
        ],
        out_specs=vmem,
        scratch_shapes=[
            pltpu.VMEM((npairs, size, size), BF16),
            pltpu.VMEM((npairs, size, size), BF16),
            pltpu.VMEM((size, size), BF16),
            pltpu.VMEM((2, size, npairs * size), BF16),
            pltpu.VMEM((size, 2 * npairs * size), BF16),
            pltpu.VMEM((2, size, npairs * size), BF16),
            pltpu.VMEM((ROOTS, 2, npairs, size, size), BF16),
            pltpu.VMEM(it2 + (nz, piece, size), BF16),
            pltpu.VMEM(it2 + (NX, chunk, size), BF16),
            pltpu.VMEM((ROOTS, NX, chunk, size), F32),
            pltpu.VMEM(it2 + (2, NX, chunk, size), BF16),
            pltpu.VMEM(it2 + (2, NX, chunk, size), BF16),
            pltpu.VMEM(it2 + (NX - 1, chunk, size), BF16),
            pltpu.VMEM(it2 + (NX - 1, chunk, size), BF16),
            pltpu.VMEM(it2 + (nz, piece, size), BF16),
            pltpu.VMEM(it2 + (nz, piece, size), BF16),
            pltpu.VMEM((chunk, size), F32),
            dma((2,)),
            dma(it2 + (nz - 1,)), dma(it2 + (nz - 1,)),
            dma(it2 + (NX - 1,)), dma(it2 + (NX - 1,)),
            dma(it2 + (2, NX)), dma(it2 + (2, NX)),
            dma(it2 + (NX - 1,)), dma(it2 + (NX - 1,)),
            dma(it2 + (nz - 1,)), dma(it2 + (nz - 1,)),
        ],
        compiler_params=pltpu.CompilerParams(
            collective_id=0, has_side_effects=True, vmem_limit_bytes=60000 * 1024
        ),
        name="sigma_twice",
    )(
        wavefunction.transpose(0, 2, 1, 3), diagonal.transpose(1, 0, 2), left_ops, right_ops, offsets.T
    )
    return result.transpose(0, 2, 1, 3)


def solution(mesh):
    in_specs = (
        P("sec", None, "op", None),
        P("sec", "op", None),
        P(("sec", "op"), None, None),
        P(("sec", "op"), None, None),
        P(("sec", "op"), None),
    )
    out_specs = P("sec", None, "op", None)
    body = functools.partial(on_device, mesh.shape["sec"], mesh.shape["op"] // NX)
    return jax.shard_map(
        body, mesh=mesh, in_specs=in_specs, out_specs=out_specs, check_vma=False
    )
```

```python
import functools

import jax
import jax.numpy as jnp
from jax import lax
from jax.experimental import pallas as pl
from jax.experimental.pallas import tpu as pltpu
from jax.sharding import PartitionSpec as P

ITERS = 2
ROOTS = 2
NX = 4
ORDER = "010100110101010100110101"
MESH = pl.DeviceIdType.MESH
F32 = jnp.float32
BF16 = jnp.bfloat16


def dot(a, b):
    return jnp.dot(a, b, preferred_element_type=F32)


def dot_nt(a, b):
    return lax.dot_general(a, b, (((1,), (1,)), ((), ())), preferred_element_type=F32)


def remote(src, dst, send, recv, device):
    return pltpu.make_async_remote_copy(
        src_ref=src, dst_ref=dst, send_sem=send, recv_sem=recv, device_id=device, device_id_type=MESH
    )


def kernel(
    ns, nz, wave, diagonal, left_hbm, right_hbm, offsets, out,
    left, right, perm, first, keep, cross, halves, pieces, rows, stay, cross_out, cross_in,
    near_out, near_in, share_out, share_in, chunk_buf,
    load_sem, gz_s, gz_r, gx_s, gx_r, y_s, y_r, xx_s, xx_r, z_s, z_r,
):
    npairs, size = left.shape[0], left.shape[1]
    chunk = size // NX
    piece = chunk // nz

    s = lax.axis_index("sec")
    o = lax.axis_index("op")
    z = o // NX
    x = o % NX
    around = tuple((x + j) % NX for j in range(NX))
    has_up, has_down = s < ns - 1, s > 0
    up_dev, down_dev = (s + 1, o), (s - 1, o)

    def z_peer(d):
        return (z + d) % nz

    def x_dev(j):
        return (s, z * NX + around[j])

    def z_dev(d):
        return (s, z_peer(d) * NX + x)

    load_l = pltpu.make_async_copy(left_hbm, left, load_sem.at[0])
    load_r = pltpu.make_async_copy(right_hbm, right, load_sem.at[1])
    load_l.start()
    load_r.start()

    for r in range(ROOTS):
        pieces[0, r, z] = wave[0].astype(F32)[:, r, :].astype(BF16)

    barrier = pltpu.get_barrier_semaphore()
    for d in range(1, nz):
        pl.semaphore_signal(barrier, inc=1, device_id=z_dev(d), device_id_type=MESH)
    for j in range(1, NX):
        pl.semaphore_signal(barrier, inc=1, device_id=x_dev(j), device_id_type=MESH)
    for other in ((s + 1) % ns, (s + ns - 1) % ns):
        pl.semaphore_signal(barrier, inc=1, device_id=(other, o), device_id_type=MESH)
    pl.semaphore_wait(barrier, nz + NX)

    x_order = sorted(range(1, NX), key=lambda j: -min(j, NX - j))
    order = sorted(range(1, nz), key=lambda d: -min(d, nz - d))

    def gz(it, r, d):
        mine, theirs = pieces.at[it, r, z], pieces.at[it, r, z_peer(nz - d)]
        return mine, mine, theirs, gz_s.at[it, r, d - 1], gz_r.at[it, r, d - 1], z_dev(d), None, None

    def gx(it, r, j):
        mine, theirs = rows.at[it, r, x], rows.at[it, r, around[NX - j]]
        return mine, mine, theirs, gx_s.at[it, r, j - 1], gx_r.at[it, r, j - 1], x_dev(j), None, None

    def yy(it, r, way, j):
        q = around[j]
        there = cross_in.at[it, r, way, q]
        device, leaves, comes = (up_dev, has_up, has_down) if way == 0 else (down_dev, has_down, has_up)
        return (
            cross_out.at[it, r, way, q], there, there,
            y_s.at[it, r, way, j], y_r.at[it, r, way, j], device, leaves, comes,
        )

    def xx(it, r, j):
        there = near_in.at[it, r, j - 1]
        return near_out.at[it, r, j - 1], there, there, xx_s.at[it, r, j - 1], xx_r.at[it, r, j - 1], x_dev(j), None, None

    def zz(it, r, d):
        return (
            share_out.at[it, r, z_peer(d)], share_in.at[it, r, z], share_in.at[it, r, z_peer(nz - d)],
            z_s.at[it, r, d - 1], z_r.at[it, r, d - 1], z_dev(d), None, None,
        )

    def act(condition, action):
        if condition is None:
            action()
        else:
            pl.when(condition)(action)

    started, received = [], set()

    def send(kind, *key):
        src, dst, _, send_sem, recv_sem, device, leaves, _ = kind(*key)
        act(leaves, lambda: remote(src, dst, send_sem, recv_sem, device).start())
        started.append((kind, key))

    def sent(kind, *key):
        src, dst, _, send_sem, recv_sem, device, leaves, _ = kind(*key)
        act(leaves, lambda: remote(src, dst, send_sem, recv_sem, device).wait_send())

    def recv(kind, *key):
        src, _, dst, send_sem, recv_sem, device, _, comes = kind(*key)
        act(comes, lambda: remote(src, dst, send_sem, recv_sem, device).wait_recv())
        received.add((kind, key))

    def gather_z_send(it, r):
        for d in order:
            send(gz, it, r, d)

    def gather_x_send(it, r):
        for d in reversed(order):
            recv(gz, it, r, d)
        for k in range(nz):
            chunk_buf[piece * k : piece * (k + 1), :] = pieces[it, r, k].astype(F32)
        rows[it, r, x] = chunk_buf[...].astype(BF16)
        for j in x_order:
            send(gx, it, r, j)

    def prepare():
        shape = (size, size)
        position = lax.broadcasted_iota(jnp.int32, shape, 0)
        column = lax.broadcasted_iota(jnp.int32, shape, 1)
        x_part = jnp.zeros(shape, jnp.int32)
        for k in range(1, NX):
            x_part = x_part + jnp.where(position >= chunk * k, 1, 0)
        inside = position - chunk * x_part
        z_part = jnp.zeros(shape, jnp.int32)
        for k in range(1, nz):
            z_part = z_part + jnp.where(inside >= piece * k, 1, 0)
        source = (inside - piece * z_part) + piece * x_part + (NX * piece) * z_part
        perm[...] = jnp.where(source == column, 1.0, 0.0).astype(BF16)
        perm_eye = jnp.where(position == column, 1.0, 0.0).astype(BF16)
        load_r.wait()
        for p in range(npairs):
            cols = slice(size * p, size * (p + 1))
            first[0, :, cols] = dot_nt(perm_eye, right[p]).astype(BF16)
            first[1, :, cols] = right[p]
        load_l.wait()
        for p in range(npairs):
            up = offsets[0, p].astype(F32)
            down = offsets[1, p].astype(F32)
            turned_rows = dot(perm[...], left[p]).astype(BF16)
            direct = dot_nt(turned_rows, perm[...])
            cols = slice(size * p, size * (p + 1))
            more = slice(size * (npairs + p), size * (npairs + p + 1))
            keep[:, cols] = (direct * (1.0 - up)).astype(BF16)
            cross[0, :, cols] = (direct * up).astype(BF16)
            transposed = dot_nt(perm[...], turned_rows)
            keep[:, more] = (transposed * (1.0 - down)).astype(BF16)
            cross[1, :, cols] = (transposed * down).astype(BF16)

        blank = jnp.zeros((NX, chunk, size), BF16)

        @pl.when(s == 0)
        def _():
            for it in range(ITERS):
                for r in range(ROOTS):
                    cross_in[it, r, 0] = blank

        @pl.when(s == ns - 1)
        def _():
            for it in range(ITERS):
                for r in range(ROOTS):
                    cross_in[it, r, 1] = blank

    def compute_cross(it, r):
        for j in reversed(x_order):
            recv(gx, it, r, j)
        vector = rows[it, r].reshape(size, size)

        for way in range(2):
            product = dot(vector, first[way]).astype(BF16)
            for p in range(npairs):
                halves[r, way, p] = product[:, size * p : size * (p + 1)]
            half_sum = dot(cross[way], halves[r, way].reshape(npairs * size, size))
            cross_out[it, r, way] = half_sum.astype(BF16).reshape(NX, chunk, size)
            for j in x_order + [0]:
                send(yy, it, r, way, j)

    def compute_own(it, r):
        own = dot(keep[...], halves[r].reshape(2 * npairs * size, size))
        stay[r] = own.reshape(NX, chunk, size)

    def total(it, r, j):
        recv(yy, it, r, 0, j)
        recv(yy, it, r, 1, j)
        q = around[j]
        return stay[r, q] + cross_in[it, r, 0, q].astype(F32) + cross_in[it, r, 1, q].astype(F32)

    def reduce_x_send(it, r):
        for j in x_order:
            near_out[it, r, j - 1] = total(it, r, j).astype(BF16)
            send(xx, it, r, j)
        stay[r, x] = total(it, r, 0)

    def reduce_z_send(it, r):
        block = stay[r, x]
        for j in reversed(x_order):
            recv(xx, it, r, j)
            block = block + near_in[it, r, j - 1].astype(F32)
        chunk_buf[...] = block
        for k in range(nz):
            share_out[it, r, k] = chunk_buf[piece * k : piece * (k + 1), :].astype(BF16)
        for d in order:
            send(zz, it, r, d)
        share_in[it, r, z] = share_out[it, r, z]

    def finish(it, r):
        for d in reversed(order):
            recv(zz, it, r, d)
        sigma = share_in[it, r, 0].astype(F32)
        for k in range(1, nz):
            sigma = sigma + share_in[it, r, k].astype(F32)
        result = sigma / diagonal[:, 0, :]
        if it < ITERS - 1:
            pieces[it + 1, r, z] = result.astype(BF16)
            gather_z_send(it + 1, r)
        else:
            results.append(result)

    steps = [functools.partial(gather_z_send, 0, r) for r in range(ROOTS)] + [prepare]
    queues = [[], []]
    for it in range(ITERS):
        for step in (
            gather_x_send, compute_cross, compute_own, reduce_x_send, reduce_z_send, finish
        ):
            for r in range(ROOTS):
                queues[r].append(functools.partial(step, it, r))
    for r in ORDER:
        steps.append(queues[int(r)].pop(0))
    results = []
    for i, step in enumerate(steps):
        if i == len(steps) - ROOTS:
            for kind, key in started:
                sent(kind, *key)
            started.clear()
        step()
    out[0] = jnp.stack(results, axis=1).astype(BF16)
    for kind, key in started:
        sent(kind, *key)


def on_device(ns, nz, wavefunction, diagonal, left_ops, right_ops, offsets):
    npairs, size, _ = left_ops.shape
    chunk = size // NX
    piece = chunk // nz
    it2 = (ITERS, ROOTS)
    dma = pltpu.SemaphoreType.DMA
    vmem = pl.BlockSpec(memory_space=pltpu.VMEM)
    result = pl.pallas_call(
        functools.partial(kernel, ns, nz),
        out_shape=jax.ShapeDtypeStruct((1, piece, ROOTS, size), BF16),
        in_specs=[
            vmem, vmem, pl.BlockSpec(memory_space=pl.ANY), pl.BlockSpec(memory_space=pl.ANY),
            pl.BlockSpec(memory_space=pltpu.SMEM),
        ],
        out_specs=vmem,
        scratch_shapes=[
            pltpu.VMEM((npairs, size, size), BF16),
            pltpu.VMEM((npairs, size, size), BF16),
            pltpu.VMEM((size, size), BF16),
            pltpu.VMEM((2, size, npairs * size), BF16),
            pltpu.VMEM((size, 2 * npairs * size), BF16),
            pltpu.VMEM((2, size, npairs * size), BF16),
            pltpu.VMEM((ROOTS, 2, npairs, size, size), BF16),
            pltpu.VMEM(it2 + (nz, piece, size), BF16),
            pltpu.VMEM(it2 + (NX, chunk, size), BF16),
            pltpu.VMEM((ROOTS, NX, chunk, size), F32),
            pltpu.VMEM(it2 + (2, NX, chunk, size), BF16),
            pltpu.VMEM(it2 + (2, NX, chunk, size), BF16),
            pltpu.VMEM(it2 + (NX - 1, chunk, size), BF16),
            pltpu.VMEM(it2 + (NX - 1, chunk, size), BF16),
            pltpu.VMEM(it2 + (nz, piece, size), BF16),
            pltpu.VMEM(it2 + (nz, piece, size), BF16),
            pltpu.VMEM((chunk, size), F32),
            dma((2,)),
            dma(it2 + (nz - 1,)), dma(it2 + (nz - 1,)),
            dma(it2 + (NX - 1,)), dma(it2 + (NX - 1,)),
            dma(it2 + (2, NX)), dma(it2 + (2, NX)),
            dma(it2 + (NX - 1,)), dma(it2 + (NX - 1,)),
            dma(it2 + (nz - 1,)), dma(it2 + (nz - 1,)),
        ],
        compiler_params=pltpu.CompilerParams(
            collective_id=0, has_side_effects=True, vmem_limit_bytes=60000 * 1024
        ),
        name="sigma_twice",
    )(
        wavefunction.transpose(0, 2, 1, 3), diagonal.transpose(1, 0, 2), left_ops, right_ops, offsets.T
    )
    return result.transpose(0, 2, 1, 3)


def solution(mesh):
    in_specs = (
        P("sec", None, "op", None),
        P("sec", "op", None),
        P(("sec", "op"), None, None),
        P(("sec", "op"), None, None),
        P(("sec", "op"), None),
    )
    out_specs = P("sec", None, "op", None)
    body = functools.partial(on_device, mesh.shape["sec"], mesh.shape["op"] // NX)
    return jax.shard_map(
        body, mesh=mesh, in_specs=in_specs, out_specs=out_specs, check_vma=False
    )
```
